256 devices in a mesh: slab: 32 (over z, x), orb: 8 (over y, core).
Axes of the slice: x: 4, y: 4, z: 8, core: 2. Of those that a mesh axis runs over, the one named last changes fastest.
Arguments:
- orbitals: bfloat16 [32, 8, 1, 64, 2304], P(None, 'orb', None, 'slab'), may hold values from -6 to 6
- potential: float32 [64, 2304], P('slab'), may hold values from -1.5 to 0.5
- partners: int32 [32, 8, 1, 2], P('slab', 'orb'), may hold values from 0 to 255, as said below
- pair_valid: int32 [32, 8, 1, 2], P('slab', 'orb'), may hold values from 0 to 1, as said below
Outputs:
- action: bfloat16 [32, 8, 1, 64, 2304], P(None, 'orb', None, 'slab')
The draws below stay inside these ranges and needn't reach their ends.
Inputs may be any that keep to these rules, and one draw needn't show every extreme that they name: partners names, for orbital number n = (a * 8 + b) + r, an orbital number that differs from n by 1 to 1 along the cyclic order of the 256 orbitals: ahead of n in even slots, behind n in odd slots; a partner may be listed more than once. `pair_valid`: slot 0 of every orbital is used.
All inputs are finite; a program needn't handle non-finite values.
Results may differ from the reference program's by a relative error of at most 0.001.
Values may be sent and summed in bfloat16 or wider, within the bound.
No kernel may reach another device: no remote copies, remote signals or barrier semaphores. Data moves between devices by JAX's collectives and lax.ppermute only.
A program may use at most 64 MiB of HBM per device.

```python
import math
import jax
import jax.numpy as jnp
from jax import lax

NX = 48
NY = 48
NZ = 64
ORB_DEV = 1
SLOTS = 2
NYX = 2304
SLABS = 32
BLOCKS = 8
NORB = 256


def draw_partners(key, part):
    size_key = jax.random.fold_in(key, 17)
    shape = (SLABS, BLOCKS, ORB_DEV, SLOTS)
    distance = jax.random.randint(size_key, shape, 1, ORB_DEV + 1)
    slot_index = jnp.arange(SLOTS, dtype=jnp.int32).reshape(1, 1, 1, SLOTS)
    direction = 1 - 2 * (slot_index % 2)
    own_number = jnp.arange(NORB, dtype=jnp.int32).reshape(SLABS, BLOCKS, ORB_DEV, 1)
    return ((own_number + direction * distance) % NORB).astype(jnp.int32)


def draw_pair_valid(key, part):
    flag_key = jax.random.fold_in(key, 29)
    shape = (SLABS, BLOCKS, ORB_DEV, SLOTS)
    drawn = (jax.random.randint(flag_key, shape, 0, 4) < 3).astype(jnp.int32)
    slot_index = jnp.arange(SLOTS, dtype=jnp.int32).reshape(1, 1, 1, SLOTS)
    return jnp.where(slot_index == 0, 1, drawn).astype(jnp.int32)


def levels(own_key, dims, cuts, smallest, top_value):
    def one(dim, shards_of):
        steps = jax.random.uniform(jax.random.fold_in(jax.random.fold_in(own_key, 6), dim), (shards_of,), jnp.float32, smallest / len(cuts), top_value / len(cuts))
        return jnp.repeat(jnp.exp(steps), dims[dim] // shards_of).reshape((-1,) + (1,) * (len(dims) - dim - 1))

    gain = one(*cuts[0])
    for cut in cuts[1:]:
        gain = gain * one(*cut)
    return gain


def gaussian(rng, extent, deviation, limit, pieces=(), held_as=jnp.bfloat16):
    entries = jax.random.normal(rng, extent, jnp.float32) * deviation
    if len(pieces) > 0:
        entries = levels(rng, extent, pieces, -0.22, 0.18) * entries
    return jnp.clip(entries, min=-limit, max=limit).astype(held_as)


def setup_inputs(seed: int = 0) -> dict:
    arg_keys = jax.random.split(jax.random.key(seed), 5)
    return {
        "orbitals": gaussian(arg_keys[0], (SLABS, BLOCKS, ORB_DEV, NZ, NYX), 1.0, 6.0, ((1, 8), (3, 32))),
        "potential": jnp.clip(-1.5 + 2.0 * jax.random.uniform(arg_keys[1], (NZ, NYX), jnp.float32) ** levels(arg_keys[1], (NZ, NYX), ((0, 32),), -0.2, 0.2), -1.5, 0.5),
        "partners": draw_partners(jax.random.fold_in(arg_keys[4], 71), 0),
        "pair_valid": draw_pair_valid(jax.random.fold_in(arg_keys[4], 71), 0),
    }


stencil_weights = (-205.0 / 72.0, 8.0 / 5.0, -1.0 / 5.0, 8.0 / 315.0, -1.0 / 560.0)
screening = 0.11
mixing = 0.25


def squared_wave(length):
    grid = jnp.arange(length, dtype=jnp.int32)
    folded = jnp.minimum(grid, length - grid).astype(jnp.float32)
    return (2.0 * math.pi * folded / length) * (2.0 * math.pi * folded / length)


def screened_kernel(depth, rows, cols):
    wave = squared_wave(depth)[:, None, None] + squared_wave(rows)[None, :, None] + squared_wave(cols)[None, None, :]
    safe = jnp.where(wave > 0, wave, 1.0)
    inner = 4.0 * math.pi / safe * (1.0 - jnp.exp(-safe / (4.0 * screening * screening)))
    return jnp.where(wave > 0, inner, math.pi / (screening * screening))


def reference(orbitals, potential, partners, pair_valid):
    total = orbitals.shape[0] * orbitals.shape[1] * orbitals.shape[2]
    values = orbitals.astype(jnp.float32).reshape(total, NZ, NY, NX)
    laplace = 3.0 * stencil_weights[0] * values
    for reach in range(1, 5):
        for axis_index in (1, 2, 3):
            laplace = laplace + stencil_weights[reach] * (jnp.roll(values, reach, axis_index) + jnp.roll(values, -reach, axis_index))
    kernel = screened_kernel(NZ, NY, NX)
    lists = partners.reshape(total, SLOTS)
    weights = pair_valid.reshape(total, SLOTS).astype(jnp.float32)

    def turn(accum, slot):
        lister = slot // SLOTS
        column = slot % SLOTS
        partner = lists[lister, column]
        weight = weights[lister, column]
        first = values[lister]
        second = values[partner]
        field = jnp.fft.ifftn(kernel * jnp.fft.fftn(first * second)).real * weight
        accum = accum.at[lister].add(field * second)
        accum = accum.at[partner].add(field * first)
        return accum, None

    slots = jnp.arange(total * SLOTS, dtype=jnp.int32)
    exchange, unused = lax.scan(turn, jnp.zeros_like(values), slots)
    grid_potential = potential.reshape(1, NZ, NY, NX)
    result = -0.5 * laplace + grid_potential * values - mixing * exchange
    return result.reshape(orbitals.shape).astype(jnp.bfloat16)
```

```python
import math

import jax
import jax.numpy as jnp
import numpy as np
from jax import lax
from jax.experimental import pallas as pl
from jax.experimental.pallas import tpu as pltpu
from jax.sharding import PartitionSpec as P

NX = 48
NY = 48
NZ = 64
NYX = NY * NX
LANES = 128
CHUNKS = NYX // LANES
GROUP = 384
REACH_LANES = 256
WINDOW = GROUP + 2 * REACH_LANES

stencil_weights = (-205.0 / 72.0, 8.0 / 5.0, -1.0 / 5.0, 8.0 / 315.0, -1.0 / 560.0)
screening = 0.11
mixing = 0.25

BF16 = jnp.bfloat16
F32 = jnp.float32


def split_table(table):
    wide = np.asarray(table, np.float32)
    high = wide.astype(jnp.bfloat16)
    low = (np.asarray(table, np.float64) - high.astype(np.float64)).astype(jnp.bfloat16)
    return high, low


def hartley(length):
    grid = np.arange(length)
    angle = (grid[:, None] * grid[None, :] % length) * (2.0 * np.pi / length)
    return np.cos(angle) + np.sin(angle)


def squared_wave(length):
    grid = np.arange(length)
    folded = np.minimum(grid, length - grid).astype(np.float64)
    return (2.0 * np.pi * folded / length) ** 2


def kernel_table():
    wave = (
        squared_wave(NX)[:, None, None]
        + squared_wave(NY)[None, :, None]
        + squared_wave(NZ)[None, None, :]
    )
    safe = np.where(wave > 0, wave, 1.0)
    inner = 4.0 * np.pi / safe * (1.0 - np.exp(-safe / (4.0 * screening * screening)))
    full = np.where(wave > 0, inner, np.pi / (screening * screening)) / (NZ * NYX)
    full = full.reshape(NX * NY, NZ)
    return np.concatenate([full, full], axis=1).astype(np.float32)


def depth_table():
    pair = np.kron(np.eye(2), hartley(NZ))
    high, low = split_table(pair)
    top = np.concatenate([high, low], axis=1)
    bottom = np.concatenate([high, np.zeros_like(low)], axis=1)
    return np.concatenate([top, bottom], axis=0)


def side_table():
    high, low = split_table(hartley(NX))
    return np.concatenate([high, high, low], axis=1)


def second_difference(length):
    table = np.zeros((length, length))
    for spot in range(length):
        table[spot, spot] += stencil_weights[0]
        for reach in range(1, 5):
            table[spot, (spot + reach) % length] += stencil_weights[reach]
            table[spot, (spot - reach) % length] += stencil_weights[reach]
    return table


def vertical_table():
    high, low = split_table(-0.5 * second_difference(NZ))
    return np.concatenate([high, low], axis=1)


def lateral_table():
    table = np.zeros((WINDOW, GROUP))
    along_x = second_difference(NX)
    for lane in range(GROUP):
        row, col = divmod(lane, NX)
        for other in range(NX):
            table[REACH_LANES + row * NX + other, lane] += along_x[col, other]
        table[REACH_LANES + lane, lane] += stencil_weights[0]
        for reach in range(1, 5):
            table[REACH_LANES + lane + reach * NX, lane] += stencil_weights[reach]
            table[REACH_LANES + lane - reach * NX, lane] += stencil_weights[reach]
    high, low = split_table(-0.5 * table)
    return np.concatenate([high, low], axis=0)


def halves(value):
    high = value.astype(BF16)
    low = (value - high.astype(F32)).astype(BF16)
    return high, low


def depth_turn(value, table):
    high, low = halves(value)
    both = jnp.dot(
        jnp.concatenate([high, low], axis=1), table, preferred_element_type=F32
    )
    return both[:, :LANES] + both[:, LANES:]


def side_turn(value, table):
    high, low = halves(value)
    return jnp.dot(
        table, jnp.concatenate([high, low, high], axis=0), preferred_element_type=F32
    )


def owner_kernel(
    flags, ahead_flags, own, ahead, behind, depth_t, side_t, wave_t, vert_t, out, work
):
    w_ahead = (flags[0, 0] + ahead_flags[0, 1]).astype(F32) * (-mixing)
    w_behind = (flags[0, 1] + 1).astype(F32) * (-mixing)
    depth = depth_t[...]
    side = side_t[...]
    vert = vert_t[...]

    for chunk in range(CHUNKS):
        cols = slice(chunk * LANES, (chunk + 1) * LANES)
        mine = own[:, cols].astype(F32)
        density = jnp.concatenate(
            [mine * ahead[:, cols].astype(F32), mine * behind[:, cols].astype(F32)], axis=0
        )
        work[cols, :] = depth_turn(density.T, depth)

    def along_x(step):
        first = slice(2 * step * NX, (2 * step + 1) * NX)
        second = slice((2 * step + 1) * NX, (2 * step + 2) * NX)
        turned = side_turn(jnp.concatenate([work[first, :], work[second, :]], axis=1), side)
        work[first, :] = turned[:, :LANES]
        work[second, :] = turned[:, LANES:]

    for step in range(NY // 2):
        along_x(step)
    for step in range(NX // 2):
        first = pl.ds(2 * step, NY, stride=NX)
        second = pl.ds(2 * step + 1, NY, stride=NX)
        turned = side_turn(jnp.concatenate([work[first, :], work[second, :]], axis=1), side)
        factor = jnp.concatenate(
            [
                wave_t[2 * step * NY : (2 * step + 1) * NY, :],
                wave_t[(2 * step + 1) * NY : (2 * step + 2) * NY, :],
            ],
            axis=1,
        )
        turned = side_turn(turned * factor, side)
        work[first, :] = turned[:, :LANES]
        work[second, :] = turned[:, LANES:]
    for step in range(NY // 2):
        along_x(step)

    for chunk in range(CHUNKS):
        cols = slice(chunk * LANES, (chunk + 1) * LANES)
        pots = depth_turn(work[cols, :], depth).T
        mine = own[:, cols]
        term = jnp.dot(vert, jnp.concatenate([mine, mine], axis=0), preferred_element_type=F32)
        term = term + w_ahead * (pots[:NZ] * ahead[:, cols].astype(F32))
        term = term + w_behind * (pots[NZ:] * behind[:, cols].astype(F32))
        high, low = halves(term)
        out[:, cols] = high
        out[:, NYX + chunk * LANES : NYX + (chunk + 1) * LANES] = low


def slab_kernel(planes, potential, lateral_t, out):
    rows = planes.shape[0]
    parity = lax.broadcasted_iota(jnp.int32, (8, GROUP), 0) % 2
    for start in range(0, NYX, GROUP):
        cols = slice(start, start + GROUP)
        pieces = []
        for lane in range(start - REACH_LANES, start + GROUP + REACH_LANES, LANES):
            at = lane % NYX
            pieces.append(planes[:, at : at + LANES])
        window = jnp.concatenate(pieces + pieces, axis=1)
        term = jnp.dot(window, lateral_t[...], preferred_element_type=F32)
        level = jnp.where(
            parity == 0,
            jnp.broadcast_to(potential[0:1, cols], (8, GROUP)),
            jnp.broadcast_to(potential[1:2, cols], (8, GROUP)),
        )
        level = jnp.concatenate([level] * (rows // 8), axis=0)
        out[:, cols] = term + level * planes[:, cols].astype(F32)


def final_kernel(base, returned, out):
    out[...] = (
        base[...] + returned[:, :NYX].astype(F32) + returned[:, NYX:].astype(F32)
    ).astype(BF16)


def vmem():
    return pl.BlockSpec(memory_space=pltpu.VMEM)


def smem():
    return pl.BlockSpec(memory_space=pltpu.SMEM)


def local(orbitals, potential, partners, pair_valid):
    count = lax.axis_size("slab")
    total = count * lax.axis_size("orb")
    to_behind = [((i + 1) % total, i) for i in range(total)]
    to_ahead = [(i, (i + 1) % total) for i in range(total)]
    chain = ("slab", "orb")
    flags = pair_valid.reshape(1, 2)
    ahead_flags = lax.ppermute(flags, chain, to_behind)
    planes = orbitals.reshape(count, 2, NYX)
    own = lax.all_to_all(planes, "slab", split_axis=0, concat_axis=0, tiled=True)
    own = own.reshape(NZ, NYX)
    ahead = lax.ppermute(own, chain, to_behind)
    behind = lax.ppermute(own, chain, to_ahead)

    base = pl.pallas_call(
        slab_kernel,
        out_shape=jax.ShapeDtypeStruct((2 * count, NYX), F32),
        in_specs=[vmem()] * 3,
        out_specs=vmem(),
        name="slab_part",
    )(planes.reshape(2 * count, NYX), potential, jnp.asarray(lateral_table()))

    terms = pl.pallas_call(
        owner_kernel,
        out_shape=jax.ShapeDtypeStruct((NZ, 2 * NYX), BF16),
        in_specs=[smem()] * 2 + [vmem()] * 7,
        out_specs=vmem(),
        scratch_shapes=[pltpu.VMEM((NYX, LANES), F32)],
        name="owner_part",
    )(
        flags,
        ahead_flags,
        own,
        ahead,
        behind,
        jnp.asarray(depth_table()),
        jnp.asarray(side_table()),
        jnp.asarray(kernel_table()),
        jnp.asarray(vertical_table()),
    )
    returned = lax.all_to_all(
        terms.reshape(count, 2, 2 * NYX), "slab", split_axis=0, concat_axis=0, tiled=True
    )
    result = pl.pallas_call(
        final_kernel,
        out_shape=jax.ShapeDtypeStruct((2 * count, NYX), BF16),
        in_specs=[vmem()] * 2,
        out_specs=vmem(),
        name="join_part",
    )(base, returned.reshape(2 * count, 2 * NYX))
    return result.reshape(orbitals.shape)


def solution(mesh):
    in_specs = (
        P(None, "orb", None, "slab", None),
        P("slab", None),
        P("slab", "orb", None, None),
        P("slab", "orb", None, None),
    )
    out_specs = P(None, "orb", None, "slab", None)
    return jax.shard_map(local, mesh=mesh, in_specs=in_specs, out_specs=out_specs, check_vma=False)
```

```python
import math

import jax
import jax.numpy as jnp
import numpy as np
from jax import lax
from jax.experimental import pallas as pl
from jax.experimental.pallas import tpu as pltpu
from jax.sharding import PartitionSpec as P

NX = 48
NY = 48
NZ = 64
NYX = NY * NX
LANES = 128
CHUNKS = NYX // LANES
GROUP = 384
REACH_LANES = 256
WINDOW = GROUP + 2 * REACH_LANES

stencil_weights = (-205.0 / 72.0, 8.0 / 5.0, -1.0 / 5.0, 8.0 / 315.0, -1.0 / 560.0)
screening = 0.11
mixing = 0.25

BF16 = jnp.bfloat16
F32 = jnp.float32


def split_table(table):
    wide = np.asarray(table, np.float32)
    high = wide.astype(jnp.bfloat16)
    low = (np.asarray(table, np.float64) - high.astype(np.float64)).astype(jnp.bfloat16)
    return high, low


def hartley(length):
    grid = np.arange(length)
    angle = (grid[:, None] * grid[None, :] % length) * (2.0 * np.pi / length)
    return np.cos(angle) + np.sin(angle)


def squared_wave(length):
    grid = np.arange(length)
    folded = np.minimum(grid, length - grid).astype(np.float64)
    return (2.0 * np.pi * folded / length) ** 2


def kernel_table():
    wave = (
        squared_wave(NX)[:, None, None]
        + squared_wave(NY)[None, :, None]
        + squared_wave(NZ)[None, None, :]
    )
    safe = np.where(wave > 0, wave, 1.0)
    inner = 4.0 * np.pi / safe * (1.0 - np.exp(-safe / (4.0 * screening * screening)))
    full = np.where(wave > 0, inner, np.pi / (screening * screening)) / (NZ * NYX)
    full = full.reshape(NX * NY, NZ)
    return np.concatenate([full, full], axis=1).astype(np.float32)


def depth_table():
    pair = np.kron(np.eye(2), hartley(NZ))
    high, low = split_table(pair)
    top = np.concatenate([high, low], axis=1)
    bottom = np.concatenate([high, np.zeros_like(low)], axis=1)
    return np.concatenate([top, bottom], axis=0)


def side_table():
    high, low = split_table(hartley(NX))
    return np.concatenate([high, high, low], axis=1)


def second_difference(length):
    table = np.zeros((length, length))
    for spot in range(length):
        table[spot, spot] += stencil_weights[0]
        for reach in range(1, 5):
            table[spot, (spot + reach) % length] += stencil_weights[reach]
            table[spot, (spot - reach) % length] += stencil_weights[reach]
    return table


def vertical_table():
    high, low = split_table(-0.5 * second_difference(NZ))
    return np.concatenate([high, low], axis=1)


def lateral_table():
    table = np.zeros((WINDOW, GROUP))
    along_x = second_difference(NX)
    for lane in range(GROUP):
        row, col = divmod(lane, NX)
        for other in range(NX):
            table[REACH_LANES + row * NX + other, lane] += along_x[col, other]
        table[REACH_LANES + lane, lane] += stencil_weights[0]
        for reach in range(1, 5):
            table[REACH_LANES + lane + reach * NX, lane] += stencil_weights[reach]
            table[REACH_LANES + lane - reach * NX, lane] += stencil_weights[reach]
    high, low = split_table(-0.5 * table)
    return np.concatenate([high, low], axis=0)


def halves(value):
    high = value.astype(BF16)
    low = (value - high.astype(F32)).astype(BF16)
    return high, low


def depth_turn(value, table):
    high, low = halves(value)
    both = jnp.dot(
        jnp.concatenate([high, low], axis=1), table, preferred_element_type=F32
    )
    return both[:, :LANES] + both[:, LANES:]


def side_turn(value, table):
    high, low = halves(value)
    return jnp.dot(
        table, jnp.concatenate([high, low, high], axis=0), preferred_element_type=F32
    )


def owner_kernel(
    flags, ahead_flags, own, ahead, behind, depth_t, side_t, wave_t, vert_t, out, work
):
    w_ahead = (flags[0, 0] + ahead_flags[0, 1]).astype(F32) * (-mixing)
    w_behind = (flags[0, 1] + 1).astype(F32) * (-mixing)
    depth = depth_t[...]
    side = side_t[...]
    vert = vert_t[...]

    for chunk in range(CHUNKS):
        cols = slice(chunk * LANES, (chunk + 1) * LANES)
        mine = own[:, cols].astype(F32)
        density = jnp.concatenate(
            [mine * ahead[:, cols].astype(F32), mine * behind[:, cols].astype(F32)], axis=0
        )
        work[cols, :] = depth_turn(density.T, depth)

    def along_x(step):
        first = slice(2 * step * NX, (2 * step + 1) * NX)
        second = slice((2 * step + 1) * NX, (2 * step + 2) * NX)
        turned = side_turn(jnp.concatenate([work[first, :], work[second, :]], axis=1), side)
        work[first, :] = turned[:, :LANES]
        work[second, :] = turned[:, LANES:]

    for step in range(NY // 2):
        along_x(step)
    for step in range(NX // 2):
        first = pl.ds(2 * step, NY, stride=NX)
        second = pl.ds(2 * step + 1, NY, stride=NX)
        turned = side_turn(jnp.concatenate([work[first, :], work[second, :]], axis=1), side)
        factor = jnp.concatenate(
            [
                wave_t[2 * step * NY : (2 * step + 1) * NY, :],
                wave_t[(2 * step + 1) * NY : (2 * step + 2) * NY, :],
            ],
            axis=1,
        )
        turned = side_turn(turned * factor, side)
        work[first, :] = turned[:, :LANES]
        work[second, :] = turned[:, LANES:]
    for step in range(NY // 2):
        along_x(step)

    for chunk in range(CHUNKS):
        cols = slice(chunk * LANES, (chunk + 1) * LANES)
        pots = depth_turn(work[cols, :], depth).T
        mine = own[:, cols]
        term = jnp.dot(vert, jnp.concatenate([mine, mine], axis=0), preferred_element_type=F32)
        term = term + w_ahead * (pots[:NZ] * ahead[:, cols].astype(F32))
        term = term + w_behind * (pots[NZ:] * behind[:, cols].astype(F32))
        high, low = halves(term)
        out[:, cols] = high
        out[:, NYX + chunk * LANES : NYX + (chunk + 1) * LANES] = low


def slab_kernel(planes, potential, lateral_t, out):
    rows = planes.shape[0]
    parity = lax.broadcasted_iota(jnp.int32, (8, GROUP), 0) % 2
    for start in range(0, NYX, GROUP):
        cols = slice(start, start + GROUP)
        pieces = []
        for lane in range(start - REACH_LANES, start + GROUP + REACH_LANES, LANES):
            at = lane % NYX
            pieces.append(planes[:, at : at + LANES])
        window = jnp.concatenate(pieces + pieces, axis=1)
        term = jnp.dot(window, lateral_t[...], preferred_element_type=F32)
        level = jnp.where(
            parity == 0,
            jnp.broadcast_to(potential[0:1, cols], (8, GROUP)),
            jnp.broadcast_to(potential[1:2, cols], (8, GROUP)),
        )
        level = jnp.concatenate([level] * (rows // 8), axis=0)
        out[:, cols] = term + level * planes[:, cols].astype(F32)


def final_kernel(base, returned, out):
    out[...] = (
        base[...] + returned[:, :NYX].astype(F32) + returned[:, NYX:].astype(F32)
    ).astype(BF16)


def vmem():
    return pl.BlockSpec(memory_space=pltpu.VMEM)


def smem():
    return pl.BlockSpec(memory_space=pltpu.SMEM)


def local(orbitals, potential, partners, pair_valid):
    count = lax.axis_size("slab")
    total = count * lax.axis_size("orb")
    to_behind = [((i + 1) % total, i) for i in range(total)]
    to_ahead = [(i, (i + 1) % total) for i in range(total)]
    chain = ("slab", "orb")
    flags = pair_valid.reshape(1, 2)
    ahead_flags = lax.ppermute(flags, chain, to_behind)
    planes = orbitals.reshape(count, 2, NYX)
    own = lax.all_to_all(planes, "slab", split_axis=0, concat_axis=0, tiled=True)
    own = own.reshape(NZ, NYX)
    ahead = lax.ppermute(own, chain, to_behind)
    behind = lax.ppermute(own, chain, to_ahead)

    base = pl.pallas_call(
        slab_kernel,
        out_shape=jax.ShapeDtypeStruct((2 * count, NYX), F32),
        in_specs=[vmem()] * 3,
        out_specs=vmem(),
        compiler_params=pltpu.CompilerParams(vmem_limit_bytes=12 << 20),
        name="slab_part",
    )(planes.reshape(2 * count, NYX), potential, jnp.asarray(lateral_table()))

    terms = pl.pallas_call(
        owner_kernel,
        out_shape=jax.ShapeDtypeStruct((NZ, 2 * NYX), BF16),
        in_specs=[smem()] * 2 + [vmem()] * 7,
        out_specs=vmem(),
        scratch_shapes=[pltpu.VMEM((NYX, LANES), F32)],
        compiler_params=pltpu.CompilerParams(vmem_limit_bytes=12 << 20),
        name="owner_part",
    )(
        flags,
        ahead_flags,
        own,
        ahead,
        behind,
        jnp.asarray(depth_table()),
        jnp.asarray(side_table()),
        jnp.asarray(kernel_table()),
        jnp.asarray(vertical_table()),
    )
    returned = lax.all_to_all(
        terms.reshape(count, 2, 2 * NYX), "slab", split_axis=0, concat_axis=0, tiled=True
    )
    result = pl.pallas_call(
        final_kernel,
        out_shape=jax.ShapeDtypeStruct((2 * count, NYX), BF16),
        in_specs=[vmem()] * 2,
        out_specs=vmem(),
        compiler_params=pltpu.CompilerParams(vmem_limit_bytes=12 << 20),
        name="join_part",
    )(base, returned.reshape(2 * count, 2 * NYX))
    return result.reshape(orbitals.shape)


def solution(mesh):
    in_specs = (
        P(None, "orb", None, "slab", None),
        P("slab", None),
        P("slab", "orb", None, None),
        P("slab", "orb", None, None),
    )
    out_specs = P(None, "orb", None, "slab", None)
    return jax.shard_map(local, mesh=mesh, in_specs=in_specs, out_specs=out_specs, check_vma=False)
```

```python
import math

import jax
import jax.numpy as jnp
import numpy as np
from jax import lax
from jax.experimental import pallas as pl
from jax.experimental.pallas import tpu as pltpu
from jax.sharding import PartitionSpec as P

NX = 48
NY = 48
NZ = 64
NYX = NY * NX
LANES = 128
CHUNKS = NYX // LANES
GROUP = 384
REACH_LANES = 256
WINDOW = GROUP + 2 * REACH_LANES
DEPTH_AT = NYX
SIDE_AT = DEPTH_AT + 512
VERT_AT = SIDE_AT + 2 * NX

CODE_RANGE = 255.0
CODE_SLOPE = 31.0
CODE_SHIFT = 124.0

stencil_weights = (-205.0 / 72.0, 8.0 / 5.0, -1.0 / 5.0, 8.0 / 315.0, -1.0 / 560.0)
screening = 0.11
mixing = 0.25

BF16 = jnp.bfloat16
F32 = jnp.float32


def split_table(table):
    wide = np.asarray(table, np.float32)
    high = wide.astype(jnp.bfloat16)
    low = (np.asarray(table, np.float64) - high.astype(np.float64)).astype(jnp.bfloat16)
    return high, low


def hartley(length):
    grid = np.arange(length)
    angle = (grid[:, None] * grid[None, :] % length) * (2.0 * np.pi / length)
    return np.cos(angle) + np.sin(angle)


def squared_wave(length):
    grid = np.arange(length)
    folded = np.minimum(grid, length - grid).astype(np.float64)
    return (2.0 * np.pi * folded / length) ** 2


def kernel_table():
    wave = (
        squared_wave(NX)[:, None, None]
        + squared_wave(NY)[None, :, None]
        + squared_wave(NZ)[None, None, :]
    )
    safe = np.where(wave > 0, wave, 1.0)
    inner = 4.0 * np.pi / safe * (1.0 - np.exp(-safe / (4.0 * screening * screening)))
    full = np.where(wave > 0, inner, np.pi / (screening * screening)) / (NZ * NYX)
    full = full.reshape(NX * NY, NZ)
    return np.concatenate([full, full], axis=1).astype(np.float32)


def depth_table():
    pair = np.kron(np.eye(2), hartley(NZ))
    high, low = split_table(pair)
    top = np.concatenate([high, low], axis=1)
    bottom = np.concatenate([high, np.zeros_like(low)], axis=1)
    return np.concatenate([top, bottom], axis=0)


def side_table():
    high, low = split_table(hartley(NX))
    return np.concatenate([high, high, low], axis=1)


def second_difference(length):
    table = np.zeros((length, length))
    for spot in range(length):
        table[spot, spot] += stencil_weights[0]
        for reach in range(1, 5):
            table[spot, (spot + reach) % length] += stencil_weights[reach]
            table[spot, (spot - reach) % length] += stencil_weights[reach]
    return table


def vertical_table():
    high, low = split_table(-0.5 * second_difference(NZ))
    return np.concatenate([high, low], axis=1)


def owner_tables():
    depth = depth_table().astype(np.float32)
    side = np.zeros((NX, 2 * LANES), np.float32)
    side[:, : 3 * NX] = side_table().astype(np.float32)
    return np.concatenate(
        [
            kernel_table(),
            depth[:, :LANES],
            depth[:, LANES:],
            side[:, :LANES],
            side[:, LANES:],
            vertical_table().astype(np.float32),
        ],
        axis=0,
    )


def lateral_table():
    table = np.zeros((WINDOW, GROUP))
    along_x = second_difference(NX)
    for lane in range(GROUP):
        row, col = divmod(lane, NX)
        for other in range(NX):
            table[REACH_LANES + row * NX + other, lane] += along_x[col, other]
        table[REACH_LANES + lane, lane] += stencil_weights[0]
        for reach in range(1, 5):
            table[REACH_LANES + lane + reach * NX, lane] += stencil_weights[reach]
            table[REACH_LANES + lane - reach * NX, lane] += stencil_weights[reach]
    high, low = split_table(-0.5 * table)
    return np.concatenate([high, low], axis=0)


def halves(value):
    high = value.astype(BF16)
    low = (value - high.astype(F32)).astype(BF16)
    return high, low


def depth_turn(value, table):
    high, low = halves(value)
    both = jnp.dot(
        jnp.concatenate([high, low], axis=1), table, preferred_element_type=F32
    )
    return both[:, :LANES] + both[:, LANES:]


def side_turn(value, table):
    high, low = halves(value)
    return jnp.dot(
        table, jnp.concatenate([high, low, high], axis=0), preferred_element_type=F32
    )


def owner_kernel(
    flags_hbm, ahead_flags, own, mate, far, tables, out, work, term_work, flags, flags_done
):
    flags_copy = pltpu.make_async_copy(flags_hbm, flags, flags_done)
    flags_copy.start()
    depth = jnp.concatenate(
        [tables[DEPTH_AT : DEPTH_AT + 256, :], tables[DEPTH_AT + 256 : SIDE_AT, :]], axis=1
    ).astype(BF16)
    side = jnp.concatenate(
        [tables[SIDE_AT : SIDE_AT + NX, :], tables[SIDE_AT + NX : VERT_AT, :]], axis=1
    )[:, : 3 * NX].astype(BF16)
    vert = tables[VERT_AT : VERT_AT + NZ, :].astype(BF16)

    for chunk in range(CHUNKS):
        cols = slice(chunk * LANES, (chunk + 1) * LANES)
        mine = own[:, cols].astype(F32)
        density = jnp.concatenate(
            [mine * mate[:, cols].astype(F32), mine * far[:, cols].astype(F32)], axis=0
        )
        work[cols, :] = depth_turn(density.T, depth)

    def along_x(step):
        first = slice(2 * step * NX, (2 * step + 1) * NX)
        second = slice((2 * step + 1) * NX, (2 * step + 2) * NX)
        turned = side_turn(jnp.concatenate([work[first, :], work[second, :]], axis=1), side)
        work[first, :] = turned[:, :LANES]
        work[second, :] = turned[:, LANES:]

    for step in range(NY // 2):
        along_x(step)
    for step in range(NX // 2):
        first = pl.ds(2 * step, NY, stride=NX)
        second = pl.ds(2 * step + 1, NY, stride=NX)
        turned = side_turn(jnp.concatenate([work[first, :], work[second, :]], axis=1), side)
        factor = jnp.concatenate(
            [
                tables[2 * step * NY : (2 * step + 1) * NY, :],
                tables[(2 * step + 1) * NY : (2 * step + 2) * NY, :],
            ],
            axis=1,
        )
        turned = side_turn(turned * factor, side)
        work[first, :] = turned[:, :LANES]
        work[second, :] = turned[:, LANES:]
    for step in range(NY // 2):
        along_x(step)

    flags_copy.wait()
    w_ahead = (flags[0, 0] + ahead_flags[0, 1]).astype(F32) * (-mixing)
    w_behind = (flags[0, 1] + 1).astype(F32) * (-mixing)
    even = lax.axis_index("orb") % 2 == 0
    w_mate = jnp.where(even, w_ahead, w_behind)
    w_far = jnp.where(even, w_behind, w_ahead)
    peak = jnp.zeros((NZ, LANES), F32)
    for chunk in range(CHUNKS):
        cols = slice(chunk * LANES, (chunk + 1) * LANES)
        pots = depth_turn(work[cols, :], depth).T
        mine = own[:, cols]
        term = jnp.dot(vert, jnp.concatenate([mine, mine], axis=0), preferred_element_type=F32)
        term = term + w_mate * (pots[:NZ] * mate[:, cols].astype(F32))
        term = term + w_far * (pots[NZ:] * far[:, cols].astype(F32))
        term_work[:, cols] = term
        peak = jnp.maximum(peak, jnp.abs(term))
    top = jnp.max(jnp.max(peak, axis=0, keepdims=True), axis=1, keepdims=True)
    scale = jnp.broadcast_to(jnp.maximum(top * 1.02, 1e-30), (NZ, LANES)).astype(BF16)
    out[:, NYX:] = scale
    inverse = CODE_RANGE / scale.astype(F32)
    for chunk in range(CHUNKS):
        cols = slice(chunk * LANES, (chunk + 1) * LANES)
        term = term_work[:, cols]
        code = jnp.exp2(jnp.log2(1.0 + jnp.abs(term) * inverse) * CODE_SLOPE - CODE_SHIFT)
        out[:, cols] = jnp.where(term < 0, -code, code).astype(BF16)


def slab_kernel(planes, potential, lateral_t, tables, own, out, tables_out):
    del tables, own, tables_out
    rows = planes.shape[0]
    parity = lax.broadcasted_iota(jnp.int32, (8, GROUP), 0) % 2
    for start in range(0, NYX, GROUP):
        cols = slice(start, start + GROUP)
        pieces = []
        for lane in range(start - REACH_LANES, start + GROUP + REACH_LANES, LANES):
            at = lane % NYX
            pieces.append(planes[:, at : at + LANES])
        window = jnp.concatenate(pieces + pieces, axis=1)
        term = jnp.dot(window, lateral_t[...], preferred_element_type=F32)
        level = jnp.where(
            parity == 0,
            jnp.broadcast_to(potential[0:1, cols], (8, GROUP)),
            jnp.broadcast_to(potential[1:2, cols], (8, GROUP)),
        )
        level = jnp.concatenate([level] * (rows // 8), axis=0)
        out[:, cols] = term + level * planes[:, cols].astype(F32)


def final_kernel(base, returned, out):
    scale = returned[:, NYX:].astype(F32) * (1.0 / CODE_RANGE)
    for chunk in range(CHUNKS):
        cols = slice(chunk * LANES, (chunk + 1) * LANES)
        code = returned[:, cols].astype(F32)
        size = jnp.exp2((jnp.log2(jnp.abs(code)) + CODE_SHIFT) * (1.0 / CODE_SLOPE)) - 1.0
        term = jnp.where(code < 0, -size, size) * scale
        out[:, cols] = (base[:, cols] + term).astype(BF16)


def vmem():
    return pl.BlockSpec(memory_space=pltpu.VMEM)


def smem():
    return pl.BlockSpec(memory_space=pltpu.SMEM)


def local(orbitals, potential, partners, pair_valid):
    count = lax.axis_size("slab")
    total = count * lax.axis_size("orb")
    chain = ("slab", "orb")
    to_behind = [((i + 1) % total, i) for i in range(total)]
    to_mate = [(i, i ^ 1) for i in range(total)]
    to_far = [(i, (i + 2 * (i % 2) - 1) % total) for i in range(total)]
    flags = pair_valid.reshape(1, 2)
    ahead_flags = lax.ppermute(flags, chain, to_behind)
    planes = orbitals.reshape(count, 2, NYX)
    own = lax.all_to_all(planes, "slab", split_axis=0, concat_axis=0, tiled=True)
    own = own.reshape(NZ, NYX)
    far = lax.ppermute(own, chain, to_far)
    mate = lax.ppermute(own, chain, to_mate)
    limits = pltpu.CompilerParams(vmem_limit_bytes=12 << 20)

    tables = jnp.asarray(owner_tables())
    base, tables = pl.pallas_call(
        slab_kernel,
        out_shape=(
            jax.ShapeDtypeStruct((2 * count, NYX), F32),
            jax.ShapeDtypeStruct(tables.shape, F32),
        ),
        in_specs=[vmem()] * 4 + [pl.BlockSpec(memory_space=pl.ANY)],
        out_specs=(vmem(), vmem()),
        input_output_aliases={3: 1},
        compiler_params=limits,
        name="slab_part",
    )(planes.reshape(2 * count, NYX), potential, jnp.asarray(lateral_table()), tables, own)

    wide = NYX + LANES
    terms = pl.pallas_call(
        owner_kernel,
        out_shape=jax.ShapeDtypeStruct((NZ, wide), BF16),
        in_specs=[pl.BlockSpec(memory_space=pltpu.HBM), smem()] + [vmem()] * 4,
        out_specs=vmem(),
        scratch_shapes=[
            pltpu.VMEM((NYX, LANES), F32),
            pltpu.VMEM((NZ, NYX), F32),
            pltpu.SMEM((1, 2), jnp.int32),
            pltpu.SemaphoreType.DMA,
        ],
        compiler_params=limits,
        name="owner_part",
    )(flags, ahead_flags, own, mate, far, tables)
    returned = lax.all_to_all(
        terms.reshape(count, 2, wide), "slab", split_axis=0, concat_axis=0, tiled=True
    )
    result = pl.pallas_call(
        final_kernel,
        out_shape=jax.ShapeDtypeStruct((2 * count, NYX), BF16),
        in_specs=[vmem()] * 2,
        out_specs=vmem(),
        compiler_params=limits,
        name="join_part",
    )(base, returned.reshape(2 * count, wide))
    return result.reshape(orbitals.shape)


def solution(mesh):
    in_specs = (
        P(None, "orb", None, "slab", None),
        P("slab", None),
        P("slab", "orb", None, None),
        P("slab", "orb", None, None),
    )
    out_specs = P(None, "orb", None, "slab", None)
    return jax.shard_map(local, mesh=mesh, in_specs=in_specs, out_specs=out_specs, check_vma=False)
```
